32 devices in a mesh: groups: 2 (over x), worker: 2 (over core), tensor: 8 (over z, y).
Axes of the slice: x: 2, y: 2, z: 4, core: 2. Of those that a mesh axis runs over, the one named last changes fastest.
Arguments:
- tokens: bfloat16 [1024, 8192], P(('groups', 'worker'), 'tensor'), parts along dimension 0, may hold values from -6 to 6
- norm_gain: float32 [8192], replicated, may hold values from 0.5 to 1.5
- query_weight: bfloat16 [8192, 8192], P(None, 'tensor'), may hold values from -0.0625 to 0.0625
- key_weight: bfloat16 [8192, 1024], P(None, 'tensor'), may hold values from -0.15625 to 0.15625
- value_weight: bfloat16 [8192, 1024], P(None, 'tensor'), may hold values from -0.0625 to 0.0625
- output_weight: bfloat16 [8192, 8192], P('tensor'), may hold values from -0.0625 to 0.0625
- cached_blocks: bfloat16 [8, 1024, 2, 1024], P(('groups', 'worker'), 'tensor'), parts along dimension 0
- cache_length: int32 [8], P('groups'), parts along dimension 0, may hold values from 256 to 1024, as said below
- block_table: int32 [8, 64], P('groups'), parts along dimension 0, may hold values from 0 to 63, each once within a row
- destination: int32 [8], P('groups'), parts along dimension 0, may hold values from 0 to 1, as said below
Outputs:
- attended: bfloat16 [4, 3, 128, 8192], P(('groups', 'worker'), None, None, 'tensor'), parts along dimension 0
The draws below stay inside these ranges and needn't reach their ends.
There are 2 independent parts, one for each index of `groups`. The reference program is written for one: setup_inputs(seed, part) draws one part's arguments, and reference() takes and returns one part's arrays. A program takes and returns all parts, laid end to end along the dimension named above; an argument that names none is the same for every part. Nothing has to cross between parts.
Inputs may be any that keep to these rules, and one draw needn't show every extreme that they name: Exactly 3 sequences have one destination, the others the other; which one is drawn. `cache_length`: some sequence has exactly 1024 cached tokens.
All inputs are finite; a program needn't handle non-finite values.
Results may differ from the reference program's by a relative error of at most 0.02.
The reference program's roundings to bfloat16 on the way count: a program that leaves them out, or rounds other values in their place, can miss the bound.
Values may be sent and summed in bfloat16 or wider, within the bound.
No kernel may reach another device: no remote copies, remote signals or barrier semaphores. Data moves between devices by JAX's collectives and lax.ppermute only.
A program may use at most 128 MiB of HBM per device.

```python
import math
import jax
import jax.numpy as jnp
from jax import lax

D = 8192
H = 64
KVH = 8
HD = 128
NEW = 128
BLK = 16
SEQS = 4
CAP = 3
CTX = 1024
NBLK = 64
N_WORKER = 2


def draw_cached_blocks(key, part):
    first, second = jax.random.split(jax.random.fold_in(key, 11), 2)
    keys_part = jax.random.normal(first, (SEQS, CTX, 1, KVH * HD), jnp.float32)
    values_part = jax.random.normal(second, (SEQS, CTX, 1, KVH * HD), jnp.float32)
    return jnp.concatenate([keys_part, values_part], axis=2).astype(jnp.bfloat16)


def draw_cache_length(key, part):
    first, second = jax.random.split(jax.random.fold_in(key, 23))
    lengths = jax.random.randint(first, (SEQS,), CTX // 4, CTX + 1)
    chosen = jax.random.randint(second, (), 0, SEQS)
    return jnp.where(jnp.arange(SEQS) == chosen, CTX, lengths).astype(jnp.int32)


def draw_destination(key, part):
    first, second = jax.random.split(jax.random.fold_in(key, 37))
    busiest = jax.random.randint(first, (), 0, 2)
    order = jax.random.permutation(second, SEQS)
    return jnp.where(order < CAP, busiest, 1 - busiest).astype(jnp.int32)


def block_levels(own_key, dims, cuts, smallest, top_value):
    loudness, own = 1.0, jax.random.fold_in(own_key, 6)
    for position, blocks in cuts:
        steps = jnp.exp(jax.random.uniform(jax.random.fold_in(own, position), (blocks,), jnp.float32, smallest / len(cuts), top_value / len(cuts)))
        loudness = loudness * jnp.repeat(steps, dims[position] // blocks).reshape([-1 if axis == position else 1 for axis in range(len(dims))])
    return loudness


def noise(rng, extent, scale, bound, cuts=(), held_as=jnp.bfloat16):
    values = jax.random.normal(rng, extent, jnp.float32) * scale
    if len(cuts) > 0:
        values = block_levels(rng, extent, cuts, -0.22, 0.18) * values
    return jnp.clip(values, min=-bound, max=bound).astype(held_as)


def setup_inputs(seed: int = 0, part: int = 0) -> dict:
    arg_keys = jax.random.split(jax.random.key(seed), 11)
    part_keys = jax.random.split(jax.random.fold_in(arg_keys[10], part), 11)
    return {
        "tokens": noise(part_keys[0], (SEQS * NEW, D), 1.0, 6.0, ((0, 2), (1, 8))),
        "norm_gain": jnp.clip(1.0 + 0.1 * jax.random.normal(arg_keys[1], (D,), jnp.float32), 0.5, 1.5),
        "query_weight": noise(arg_keys[2], (D, H * HD), D ** -0.5, 0.0625, ((1, 8),)),
        "key_weight": noise(arg_keys[3], (D, KVH * HD), (D // 6) ** -0.5, 0.15625, ((1, 8),)),
        "value_weight": noise(arg_keys[4], (D, KVH * HD), D ** -0.5, 0.0625, ((1, 8),)),
        "output_weight": noise(arg_keys[5], (H * HD, D), (H * HD) ** -0.5, 0.0625, ((0, 8),)),
        "cached_blocks": draw_cached_blocks(jax.random.fold_in(jax.random.fold_in(arg_keys[10], part), 71), part),
        "cache_length": draw_cache_length(jax.random.fold_in(jax.random.fold_in(arg_keys[10], part), 71), part),
        "block_table": jax.vmap(lambda own: jax.random.permutation(own, NBLK))(jax.random.split(part_keys[8], SEQS)).reshape((SEQS, NBLK)).astype(jnp.int32),
        "destination": draw_destination(jax.random.fold_in(jax.random.fold_in(arg_keys[10], part), 71), part),
    }


epsilon = 1e-05

def rotate(values, positions):
    halfway = HD // 2
    inverse = 500000.0 ** (-(jnp.arange(halfway, dtype=jnp.float32) * 2.0 / HD))
    angles = positions[:, None] * inverse[None, :]
    cosine_table = jnp.concatenate([jnp.cos(angles), jnp.cos(angles)], axis=-1)[:, None, :]
    sine_table = jnp.concatenate([jnp.sin(angles), jnp.sin(angles)], axis=-1)[:, None, :]
    turned = jnp.concatenate([-values[..., halfway:], values[..., :halfway]], axis=-1)
    return values * cosine_table + turned * sine_table

def reference(tokens, norm_gain, query_weight, key_weight, value_weight, output_weight, cached_blocks, cache_length, block_table, destination):
    group_size = H // KVH

    def single(index):
        rows = lax.dynamic_slice_in_dim(tokens, index * NEW, NEW, 0).astype(jnp.float32)
        factor = lax.rsqrt(lax.optimization_barrier(jnp.mean(rows * rows, axis=1)) + epsilon)[:, None]
        scaled = (rows * norm_gain[None, :]).astype(jnp.bfloat16)
        positions = (cache_length[index] + jnp.arange(NEW, dtype=jnp.int32)).astype(jnp.float32)
        query = jnp.dot(scaled, query_weight, preferred_element_type=jnp.float32) * factor
        query = rotate(query.reshape(NEW, H, HD), positions).astype(jnp.bfloat16)
        key_raw = (jnp.dot(scaled, key_weight, preferred_element_type=jnp.float32) * factor).astype(jnp.bfloat16)
        key_raw = lax.optimization_barrier(key_raw)
        value = (jnp.dot(scaled, value_weight, preferred_element_type=jnp.float32) * factor).astype(jnp.bfloat16)
        key = rotate(key_raw.astype(jnp.float32).reshape(NEW, KVH, HD), positions).astype(jnp.bfloat16)
        value = value.reshape(NEW, KVH, HD)
        stored = lax.dynamic_index_in_dim(cached_blocks, index, 0, keepdims=False)
        old_key = stored[:, 0, :].reshape(CTX, KVH, HD)
        old_value = stored[:, 1, :].reshape(CTX, KVH, HD)
        slots = jnp.arange(CTX, dtype=jnp.int32)
        table_row = lax.dynamic_index_in_dim(block_table, index, 0, keepdims=False)
        logical = jnp.take(table_row, slots // BLK) * BLK + slots % BLK
        visible = logical < cache_length[index]
        causal = jnp.arange(NEW)[:, None] >= jnp.arange(NEW)[None, :]
        allowed = jnp.concatenate([jnp.broadcast_to(visible[None, :], (NEW, CTX)), causal], axis=1)
        all_keys = jnp.concatenate([old_key, key], axis=0).astype(jnp.float32)
        all_values = jnp.concatenate([old_value, value], axis=0).astype(jnp.float32)
        grouped = query.reshape(NEW, KVH, group_size, HD).astype(jnp.float32)
        scores = jnp.einsum('qhgd,khd->hgqk', grouped, all_keys) / math.sqrt(HD)
        scores = jnp.where(allowed[None, None], scores, -1e+30)
        largest = lax.optimization_barrier(jnp.max(scores, axis=3, keepdims=True))
        expo = jnp.exp(scores - largest)
        weights = (expo / lax.optimization_barrier(jnp.sum(expo, axis=3, keepdims=True))).astype(jnp.bfloat16)
        mixture = jnp.einsum('hgqk,khd->qhgd', weights.astype(jnp.float32), all_values)
        mixture = mixture.astype(jnp.bfloat16).reshape(NEW, H * HD)
        return jnp.dot(mixture, output_weight, preferred_element_type=jnp.float32).astype(jnp.bfloat16)
    finished = lax.map(single, jnp.arange(SEQS, dtype=jnp.int32))
    placed_all = []
    for worker_id in range(N_WORKER):
        belongs = (destination == worker_id).astype(jnp.int32)
        ranking = jnp.cumsum(belongs) - 1
        matched = (belongs[None, :] == 1) & (ranking[None, :] == jnp.arange(CAP, dtype=jnp.int32)[:, None])
        owner = lax.optimization_barrier(jnp.sum(matched.astype(jnp.int32) * jnp.arange(SEQS, dtype=jnp.int32)[None, :], axis=1))
        occupied = jnp.any(matched, axis=1)
        picked = jnp.take(finished, owner, axis=0)
        placed_all.append(jnp.where(occupied[:, None, None], picked, jnp.zeros_like(picked)))
    return jnp.stack(placed_all)
```

```python
import math

import jax
import jax.numpy as jnp
from jax import lax
from jax.experimental import pallas as pl
from jax.experimental.pallas import tpu as pltpu
from jax.sharding import PartitionSpec as P

D = 8192
KVH = 8
HD = 128
NEW = 128
BLK = 16
CAP = 3


epsilon = 1e-05
hidden = -1e30
wide = jnp.float32
narrow = jnp.bfloat16


def tables_of(positions):
    halfway = HD // 2
    inverse = 500000.0 ** (-(jnp.arange(halfway, dtype=wide) * 2.0 / HD))
    angles = positions[..., None] * inverse
    cosine, sine = jnp.cos(angles), jnp.sin(angles)
    return (
        jnp.concatenate([cosine, cosine], axis=-1),
        jnp.concatenate([-sine, sine], axis=-1),
    )


class Plane:
    def __init__(self, count):
        self.count = count
        self.near = [(i, i ^ 1) for i in range(count)]
        self.pair = [(i, i ^ 2) for i in range(count)]
        middle = [(2, 4), (3, 5)]
        edge = [(2, 0), (3, 1), (4, 6), (5, 7)]
        self.middle = middle + [(b, a) for a, b in middle]
        self.outward = edge
        self.inward = [(b, a) for a, b in edge]
        far = lax.axis_index("tensor") // 2
        self.central = (far == 1) | (far == 2)

    def send(self, block, route):
        return lax.ppermute(block, "tensor", route)

    def gather(self, own):
        from_pair = self.send(own, self.pair)
        across = self.send(own, self.middle)
        near_own = self.send(own, self.near)
        across_pair = self.send(from_pair, self.middle)
        near_pair = self.send(from_pair, self.near)
        relayed = self.send(across, self.outward)
        third = jnp.where(self.central, across, relayed)
        near_third = self.send(third, self.near)
        relayed_pair = self.send(across_pair, self.outward)
        fourth = jnp.where(self.central, across_pair, relayed_pair)
        near_fourth = self.send(fourth, self.near)
        return [own, near_own, from_pair, near_pair, third, near_third, fourth, near_fourth]

    def offsets(self):
        six = jnp.where(self.central, 6, 4)
        four = jnp.where(self.central, 4, 6)
        return jnp.stack([jnp.int32(v) for v in (0, 1, 2, 3)] + [six, six ^ 1, four, four ^ 1])

    def scatter(self, blocks):
        part = {}
        for far in (3, 2, 1, 0):
            other = self.send(blocks[2 * far + 1], self.near)
            part[far] = blocks[2 * far].astype(wide) + other.astype(wide)
        inbound_far = self.send(part[3].astype(narrow), self.inward)
        inbound_two = self.send(part[2].astype(narrow), self.inward)
        to_pair = (part[2] + inbound_far.astype(wide)).astype(narrow)
        crossed_pair = self.send(to_pair, self.middle)
        to_cross = (part[3] + inbound_two.astype(wide)).astype(narrow)
        crossed = self.send(to_cross, self.middle)
        last = (part[1] + crossed_pair.astype(wide)).astype(narrow)
        from_pair = self.send(last, self.pair)
        return (part[0] + from_pair.astype(wide) + crossed.astype(wide)).astype(narrow)

    def exchange(self, pieces):
        index = lax.axis_index("tensor")
        rest = pieces.shape[1:]
        grid = pieces.reshape((self.count // 2, 2) + rest)
        keep = lax.dynamic_index_in_dim(grid, index % 2, 1, keepdims=False)
        give = lax.dynamic_index_in_dim(grid, 1 - index % 2, 1, keepdims=False)
        taken = self.send(give, self.near)
        arrived = []
        for far in range(self.count // 2):
            target = index // 2 ^ far
            block = jnp.stack(
                [
                    lax.dynamic_index_in_dim(keep, target, 0, keepdims=False),
                    lax.dynamic_index_in_dim(taken, target, 0, keepdims=False),
                ]
            )
            if far:
                block = self.send(block, [(i, i ^ 2 * far) for i in range(self.count)])
            arrived.append(block)
        return arrived


def project(chunks, sources, gain, query_weight, key_weight, value_weight, cosine, sine):
    count = len(chunks)
    rows, width = chunks[0].shape
    query_cols = query_weight.shape[1]
    key_cols = key_weight.shape[1]
    heads = query_cols // HD

    def body(source_ref, *refs):
        chunk_refs = refs[:count]
        gain_ref, query_hbm, key_hbm, value_hbm, cosine_ref, sine_ref = refs[count : count + 6]
        query_out, key_out, value_out = refs[count + 6 : count + 9]
        query_buf, key_buf, value_buf, query_acc, key_acc, value_acc, sems = refs[count + 9 :]
        copies = []
        for step in range(count):
            start = source_ref[step] * width
            group = [
                pltpu.make_async_copy(hbm.at[pl.ds(start, width), :], buf.at[step], sems.at[k, step])
                for k, (hbm, buf) in enumerate(
                    ((query_hbm, query_buf), (key_hbm, key_buf), (value_hbm, value_buf))
                )
            ]
            for copy in group:
                copy.start()
            copies.append(group)
        squares = jnp.zeros((rows, 1), wide)
        for step in range(count):
            values = chunk_refs[step][...].astype(wide)
            squares = squares + jnp.sum(values * values, axis=1, keepdims=True)
            scaled = (values * gain_ref[source_ref[step]]).astype(narrow)
            for copy in copies[step]:
                copy.wait()
            for acc, buf in ((query_acc, query_buf), (key_acc, key_buf), (value_acc, value_buf)):
                product = jnp.dot(scaled, buf[step], preferred_element_type=wide)
                if step:
                    acc[...] += product
                else:
                    acc[...] = product
        factor = lax.rsqrt(squares / D + epsilon)
        cosines, sines = cosine_ref[...], sine_ref[...]
        for head in range(heads):
            raw = query_acc[:, head * HD : (head + 1) * HD] * factor
            turned = pltpu.roll(raw, HD // 2, axis=1)
            query_out[head] = (raw * cosines + turned * sines).astype(narrow)
        key_out[...] = (key_acc[...] * factor).astype(narrow)
        value_out[...] = (value_acc[...] * factor).astype(narrow)

    vmem = pl.BlockSpec(memory_space=pltpu.VMEM)
    hbm = pl.BlockSpec(memory_space=pl.ANY)
    return pl.pallas_call(
        body,
        out_shape=(
            jax.ShapeDtypeStruct((heads, rows, HD), narrow),
            jax.ShapeDtypeStruct((rows, key_cols), narrow),
            jax.ShapeDtypeStruct((rows, key_cols), narrow),
        ),
        in_specs=[pl.BlockSpec(memory_space=pltpu.SMEM)]
        + [vmem] * count
        + [vmem, hbm, hbm, hbm, vmem, vmem],
        out_specs=(vmem, vmem, vmem),
        scratch_shapes=[
            pltpu.VMEM((count, width, query_cols), narrow),
            pltpu.VMEM((count, width, key_cols), narrow),
            pltpu.VMEM((count, width, key_cols), narrow),
            pltpu.VMEM((rows, query_cols), wide),
            pltpu.VMEM((rows, key_cols), wide),
            pltpu.VMEM((rows, key_cols), wide),
            pltpu.SemaphoreType.DMA((3, count)),
        ],
        name="project",
    )(sources, *chunks, gain, query_weight, key_weight, value_weight, cosine, sine)


def attend_and_mix(index, sequence, query, key_raw, value, cosine, sine, visible, stored, weight):
    heads, rows, _ = query.shape
    fars = len(stored)
    local_tokens = stored[0].shape[3]
    devices = 2 * fars
    context = devices * local_tokens
    cols = weight.shape[1] // devices
    inner = weight.shape[0]
    root = 1.0 / math.sqrt(HD)

    def body(index_ref, query_ref, key_ref, value_ref, cosine_ref, sine_ref, visible_ref, *refs):
        stored_refs = refs[:fars]
        weight_hbm = refs[fars]
        outs = refs[fars + 1 : fars + 1 + devices]
        weight_buf, keys, values, mixed, staged, sems, out_sems = refs[fars + 1 + devices :]
        here = index_ref[0]
        order = [2 * far + near for far in reversed(range(fars)) for near in (1, 0)]
        loads = {}
        for slot in order:
            loads[slot] = pltpu.make_async_copy(
                weight_hbm.at[:, pl.ds((here ^ slot) * cols, cols)], weight_buf.at[slot], sems.at[slot]
            )
            loads[slot].start()
        for far in range(fars):
            for near in (0, 1):
                start = (here ^ (2 * far + near)) * local_tokens
                keys[pl.ds(start, local_tokens), :] = stored_refs[far][near, 0, 0]
                values[pl.ds(start, local_tokens), :] = stored_refs[far][near, 0, 1]
        raw = key_ref[...].astype(wide)
        turned = pltpu.roll(raw, HD // 2, axis=1)
        new_key = (raw * cosine_ref[...] + turned * sine_ref[...]).astype(narrow)
        new_value = value_ref[...]
        seen = visible_ref[...] > 0
        causal = lax.broadcasted_iota(jnp.int32, (rows, rows), 0) >= lax.broadcasted_iota(
            jnp.int32, (rows, rows), 1
        )
        across = (((1,), (1,)), ((), ()))
        for head in range(heads):
            own = query_ref[head]
            old = lax.dot_general(own, keys[...], across, preferred_element_type=wide) * root
            old = jnp.where(seen, old, hidden)
            new = lax.dot_general(own, new_key, across, preferred_element_type=wide) * root
            new = jnp.where(causal, new, hidden)
            largest = jnp.maximum(
                jnp.max(old, axis=1, keepdims=True), jnp.max(new, axis=1, keepdims=True)
            )
            old = jnp.exp(old - largest)
            new = jnp.exp(new - largest)
            total = jnp.sum(old, axis=1, keepdims=True) + jnp.sum(new, axis=1, keepdims=True)
            share = 1.0 / total
            mix = jnp.dot((old * share).astype(narrow), values[...], preferred_element_type=wide)
            mix = mix + jnp.dot((new * share).astype(narrow), new_value, preferred_element_type=wide)
            mixed[:, head * HD : (head + 1) * HD] = mix.astype(narrow)
        stores = []
        for slot in order:
            loads[slot].wait()
            product = jnp.dot(mixed[...], weight_buf[slot], preferred_element_type=wide)
            staged[slot] = product.astype(narrow)
            store = pltpu.make_async_copy(staged.at[slot], outs[slot], out_sems.at[slot])
            store.start()
            stores.append(store)
        for store in stores:
            store.wait()

    vmem = pl.BlockSpec(memory_space=pltpu.VMEM)
    hbm = pl.BlockSpec(memory_space=pl.ANY)
    piece = pl.BlockSpec((2, 1, 2, local_tokens, HD), lambda i: (0, sequence, 0, 0, 0))

    def whole(array):
        return pl.BlockSpec(array.shape, lambda i, n=array.ndim: (0,) * n)

    return pl.pallas_call(
        body,
        grid=(1,),
        out_shape=[jax.ShapeDtypeStruct((rows, cols), narrow)] * devices,
        in_specs=[pl.BlockSpec(memory_space=pltpu.SMEM)]
        + [whole(a) for a in (query, key_raw, value, cosine, sine, visible)]
        + [piece] * fars
        + [hbm],
        out_specs=[hbm] * devices,
        scratch_shapes=[
            pltpu.VMEM((devices, inner, cols), narrow),
            pltpu.VMEM((context, HD), narrow),
            pltpu.VMEM((context, HD), narrow),
            pltpu.VMEM((rows, inner), narrow),
            pltpu.VMEM((devices, rows, cols), narrow),
            pltpu.SemaphoreType.DMA((devices,)),
            pltpu.SemaphoreType.DMA((devices,)),
        ],
        name="attend_and_mix",
    )(index, query, key_raw, value, cosine, sine, visible, *stored, weight)


def attend_on_plane(
    token_rows,
    blocks,
    lengths,
    tables,
    norm_gain,
    query_weight,
    key_weight,
    value_weight,
    output_weight,
):
    count = lax.axis_size("tensor")
    index = lax.axis_index("tensor")
    plane = Plane(count)
    seq_count, local_tokens = blocks.shape[0], blocks.shape[1]
    width = token_rows.shape[1]
    logical = tables[:, :, None] * BLK + jnp.arange(BLK, dtype=jnp.int32)
    logical = logical.reshape(seq_count, 1, -1)
    visible = (logical < lengths[:, None, None]).astype(wide)
    positions = (lengths[:, None] + jnp.arange(NEW, dtype=jnp.int32)[None, :]).astype(wide)
    cosine, sine = tables_of(positions)
    gain = norm_gain.reshape(count, 1, width)
    sources = index ^ plane.offsets()
    pieces = blocks.reshape(seq_count, local_tokens, 2, count, HD).transpose(3, 0, 2, 1, 4)
    rows = token_rows.reshape(seq_count, NEW, width)
    chunks = [plane.gather(rows[s]) for s in range(seq_count)]
    stored = plane.exchange(pieces)
    results = []
    for s in range(seq_count):
        query, key_raw, value = project(
            chunks[s], sources, gain, query_weight, key_weight, value_weight, cosine[s], sine[s]
        )
        partial = attend_and_mix(
            index[None], s, query, key_raw, value, cosine[s], sine[s], visible[s], stored, output_weight
        )
        results.append(plane.scatter(partial))
    return results


def fits_plane(count):
    return count == KVH and count == 2 * 4


def from_partner(block, axis, bit):
    count = lax.axis_size(axis)
    route = []
    for low in range(count):
        high = low | 1 << bit
        if high != low and high < count:
            route += [(low, high), (high, low)]
    return lax.ppermute(block, axis, route)


def rotate(values, positions):
    halfway = HD // 2
    inverse = 500000.0 ** (-(jnp.arange(halfway, dtype=jnp.float32) * 2.0 / HD))
    angles = positions[:, None] * inverse[None, :]
    cosine_table = jnp.concatenate([jnp.cos(angles), jnp.cos(angles)], axis=-1)[:, None, :]
    sine_table = jnp.concatenate([jnp.sin(angles), jnp.sin(angles)], axis=-1)[:, None, :]
    turned = jnp.concatenate([-values[..., halfway:], values[..., :halfway]], axis=-1)
    return values * cosine_table + turned * sine_table


def attend_anywhere(
    token_rows,
    blocks,
    lengths,
    tables,
    norm_gain,
    query_weight,
    key_weight,
    value_weight,
    output_weight,
):
    tensor_count = lax.axis_size("tensor")
    tensor_index = lax.axis_index("tensor")
    group_width = tensor_count // KVH
    bit_count = group_width.bit_length() - 1
    seq_count = blocks.shape[0]
    total = token_rows.shape[0]
    query_cols = query_weight.shape[1]
    widened = lax.all_gather(token_rows, "tensor", axis=1, tiled=True).astype(jnp.float32)
    scaled = (widened * norm_gain[None, :]).astype(jnp.bfloat16)
    query_sum = jnp.dot(scaled, query_weight, preferred_element_type=jnp.float32)
    key_sum = jnp.dot(scaled, key_weight, preferred_element_type=jnp.float32)
    value_sum = jnp.dot(scaled, value_weight, preferred_element_type=jnp.float32)
    squares = jnp.sum(widened * widened, axis=1)
    factor = lax.rsqrt(squares / D + epsilon)[:, None]
    positions = (
        (lengths[:, None] + jnp.arange(NEW, dtype=jnp.int32)[None, :])
        .reshape(total)
        .astype(jnp.float32)
    )
    heads_here = query_cols // HD
    queries = rotate((query_sum * factor).reshape(total, heads_here, HD), positions).astype(
        jnp.bfloat16
    )
    key_full = (key_sum * factor).astype(jnp.bfloat16)
    value_full = (value_sum * factor).astype(jnp.bfloat16)
    for bit in range(bit_count):
        other_key, other_value = from_partner((key_full, value_full), "tensor", bit)
        upper = tensor_index // (1 << bit) % 2 == 1
        key_full = jnp.where(
            upper,
            jnp.concatenate([other_key, key_full], axis=1),
            jnp.concatenate([key_full, other_key], axis=1),
        )
        value_full = jnp.where(
            upper,
            jnp.concatenate([other_value, value_full], axis=1),
            jnp.concatenate([value_full, other_value], axis=1),
        )
    new_key = rotate(key_full.astype(jnp.float32)[:, None, :], positions)[:, 0, :].astype(
        jnp.bfloat16
    )
    fresh_keys = new_key.reshape(seq_count, NEW, HD)
    fresh_values = value_full.reshape(seq_count, NEW, HD)
    local_tokens = blocks.shape[1]
    inverse_root = 1.0 / math.sqrt(HD)
    query_blocks = queries.reshape(seq_count, NEW, heads_here, HD)
    causal = jnp.arange(NEW)[:, None] >= jnp.arange(NEW)[None, :]
    spread = jnp.repeat(
        blocks.reshape(seq_count, local_tokens, 2, KVH, HD), tensor_count // KVH, axis=3
    )
    arrived = lax.all_to_all(spread, "tensor", split_axis=3, concat_axis=1, tiled=True)
    context = arrived.shape[1]
    old_key = arrived[:, :, 0, 0, :]
    old_value = arrived[:, :, 1, 0, :]
    logical = (tables[:, :, None] * BLK + jnp.arange(BLK, dtype=jnp.int32)).reshape(seq_count, context)
    visible = logical < lengths[:, None]
    old_scores = (
        jnp.einsum("sqhd,skd->shqk", query_blocks, old_key, preferred_element_type=jnp.float32)
        * inverse_root
    )
    old_scores = jnp.where(visible[:, None, None, :], old_scores, -1e30)
    new_scores = (
        jnp.einsum("sqhd,skd->shqk", query_blocks, fresh_keys, preferred_element_type=jnp.float32)
        * inverse_root
    )
    new_scores = jnp.where(causal[None, None], new_scores, -1e30)
    largest = jnp.maximum(jnp.max(old_scores, axis=3), jnp.max(new_scores, axis=3))[..., None]
    old_expo = jnp.exp(old_scores - largest)
    new_expo = jnp.exp(new_scores - largest)
    denominator = (jnp.sum(old_expo, axis=3) + jnp.sum(new_expo, axis=3))[..., None]
    old_probs = (old_expo / denominator).astype(jnp.bfloat16)
    new_probs = (new_expo / denominator).astype(jnp.bfloat16)
    mixture = jnp.einsum("shqk,skd->sqhd", old_probs, old_value, preferred_element_type=jnp.float32)
    mixture = mixture + jnp.einsum(
        "shqk,skd->sqhd", new_probs, fresh_values, preferred_element_type=jnp.float32
    )
    attended_rows = mixture.astype(jnp.bfloat16).reshape(total, heads_here * HD)
    partial_value = jnp.dot(attended_rows, output_weight, preferred_element_type=jnp.float32)
    summed = lax.psum_scatter(partial_value, "tensor", scatter_dimension=1, tiled=True)
    finished = summed.astype(jnp.bfloat16).reshape(seq_count, NEW, -1)
    return [finished[s] for s in range(seq_count)]


def local(
    tokens,
    norm_gain,
    query_weight,
    key_weight,
    value_weight,
    output_weight,
    cached_blocks,
    cache_length,
    block_table,
    destination,
):
    worker_index = lax.axis_index("worker")
    worker_count = lax.axis_size("worker")
    seq_total = destination.shape[0]
    belongs = (destination == worker_index).astype(jnp.int32)
    ranking = jnp.sum(jnp.tril(jnp.broadcast_to(belongs, (seq_total, seq_total))), axis=1) - 1
    matched = (belongs[None, :] == 1) & (
        ranking[None, :] == jnp.arange(CAP, dtype=jnp.int32)[:, None]
    )
    local_count = cached_blocks.shape[0]
    first = worker_index * local_count
    run = attend_on_plane if fits_plane(lax.axis_size("tensor")) else attend_anywhere
    own = run(
        tokens,
        cached_blocks,
        lax.dynamic_slice_in_dim(cache_length, first, local_count, 0),
        lax.dynamic_slice_in_dim(block_table, first, local_count, 0),
        norm_gain,
        query_weight,
        key_weight,
        value_weight,
        output_weight,
    )
    slots = [jnp.zeros_like(own[0]) for _ in range(CAP)]
    for shift in range(worker_count):
        route = [(w, (w + shift) % worker_count) for w in range(worker_count)]
        start = (worker_index - shift) % worker_count * local_count
        taken = lax.dynamic_slice_in_dim(matched, start, local_count, 1)
        for s in range(local_count):
            block = lax.ppermute(own[s], "worker", route) if shift else own[s]
            for k in range(CAP):
                slots[k] = jnp.where(taken[k, s], block, slots[k])
    return jnp.stack(slots)[None]


def solution(mesh):
    placed = (
        P(("groups", "worker"), "tensor"),
        P(),
        P(None, "tensor"),
        P(None, "tensor"),
        P(None, "tensor"),
        P("tensor", None),
        P(("groups", "worker"), "tensor", None, None),
        P("groups"),
        P("groups", None),
        P("groups"),
    )
    return jax.shard_map(
        local,
        mesh=mesh,
        in_specs=placed,
        out_specs=P(("groups", "worker"), None, None, "tensor"),
        check_vma=False,
    )
```

```python
import math

import jax
import jax.numpy as jnp
from jax import lax
from jax.experimental import pallas as pl
from jax.experimental.pallas import tpu as pltpu
from jax.sharding import PartitionSpec as P


D = 8192
KVH = 8
HD = 128
NEW = 128
BLK = 16
CAP = 3


epsilon = 1e-05
hidden = -1e30
wide = jnp.float32
narrow = jnp.bfloat16


def tables_of(positions):
    halfway = HD // 2
    inverse = 500000.0 ** (-(jnp.arange(halfway, dtype=wide) * 2.0 / HD))
    angles = positions[..., None] * inverse
    cosine, sine = jnp.cos(angles), jnp.sin(angles)
    return (
        jnp.concatenate([cosine, cosine], axis=-1),
        jnp.concatenate([-sine, sine], axis=-1),
    )


def added(*terms):
    total = terms[0].astype(wide)
    for term in terms[1:]:
        total = total + term.astype(wide)
    return total.astype(narrow)


class Plane:
    def __init__(self, count):
        self.count = count
        self.fars = count // 2
        self.middle = [(2, 4), (3, 5), (4, 2), (5, 3)]
        self.outward = [(2, 0), (3, 1), (4, 6), (5, 7)]

    def send(self, block, offset):
        route = [(i, i ^ offset) for i in range(self.count)]
        return lax.ppermute(block, "tensor", route)

    def pass_on(self, block, route):
        return lax.ppermute(block, "tensor", route)

    def relay(self, own):
        middle, outward = self.middle, self.outward
        far = lax.axis_index("tensor") // 2
        central = (far == 1) | (far == 2)
        paired = self.send(own, 2)
        crossed = self.pass_on(own, middle)
        crossed_pair = self.pass_on(paired, middle)
        third = jnp.where(central, crossed, self.pass_on(crossed, outward))
        fourth = jnp.where(central, crossed_pair, self.pass_on(crossed_pair, outward))
        direct = [own, paired, third, fourth]
        near = [self.send(block, 1) for block in direct]
        blocks = [block for both in zip(direct, near) for block in both]
        late = jnp.where(central, jnp.int32(6), jnp.int32(4))
        order = [jnp.int32(k) for k in range(4)] + [late, late ^ 1, late ^ 2, late ^ 3]
        return blocks, jnp.stack(order)

    def swap(self, blocks):
        return {
            far: (blocks[2 * far], self.send(blocks[2 * far + 1], 1))
            for far in reversed(range(self.fars))
        }

    def scatter(self, blocks):
        part = self.swap(blocks)
        sums = [self.send(added(*part[far]), 2 * far) for far in (3, 2, 1)]
        return added(*part[0], *sums)

    def exchange(self, pieces):
        index = lax.axis_index("tensor")
        taken = []
        for k in range(self.count):
            block = lax.dynamic_index_in_dim(pieces, index ^ k, 0, keepdims=False)
            taken.append(self.send(block, k) if k else block)
        return taken


def project(chunks, sources, carry, gain, weights, cosine, sine):
    count = len(chunks)
    rows, width = chunks[0].shape
    query_cols, key_cols = weights[0].shape[1], weights[1].shape[1]
    heads = query_cols // HD
    carried = () if carry is None else tuple(carry)
    tables = () if cosine is None else (cosine, sine)
    sums = [
        jax.ShapeDtypeStruct((rows, query_cols), wide),
        jax.ShapeDtypeStruct((rows, key_cols), wide),
        jax.ShapeDtypeStruct((rows, key_cols), wide),
        jax.ShapeDtypeStruct((rows, 1), wide),
    ]
    finals = [
        jax.ShapeDtypeStruct((heads, rows, HD), narrow),
        jax.ShapeDtypeStruct((rows, key_cols), narrow),
        jax.ShapeDtypeStruct((rows, key_cols), narrow),
    ]

    def body(source_ref, *refs):
        refs = list(refs)

        def take(number):
            taken, refs[:number] = refs[:number], []
            return taken

        chunk_refs = take(count)
        (gain_ref,) = take(1)
        weight_refs = take(3)
        carry_refs = take(len(carried))
        table_refs = take(len(tables))
        outs = take(3 if tables else 4)
        bufs = take(3)
        accs = take(3) if tables else outs[:3]
        (sems,) = refs
        copies = []
        for step in range(count):
            start = source_ref[step] * width
            group = [
                pltpu.make_async_copy(hbm.at[pl.ds(start, width), :], buf.at[step], sems.at[k, step])
                for k, (hbm, buf) in enumerate(zip(weight_refs, bufs))
            ]
            for copy in group:
                copy.start()
            copies.append(group)
        squares = carry_refs[3][...] if carried else jnp.zeros((rows, 1), wide)
        for step in range(count):
            values = chunk_refs[step][...].astype(wide)
            squares = squares + jnp.sum(values * values, axis=1, keepdims=True)
            scaled = (values * gain_ref[source_ref[step]]).astype(narrow)
            for copy in copies[step]:
                copy.wait()
            for k, (acc, buf) in enumerate(zip(accs, bufs)):
                product = jnp.dot(scaled, buf[step], preferred_element_type=wide)
                if step:
                    acc[...] += product
                elif carried:
                    acc[...] = carry_refs[k][...] + product
                else:
                    acc[...] = product
        if not tables:
            outs[3][...] = squares
            return
        factor = lax.rsqrt(squares / D + epsilon)
        cosines, sines = table_refs[0][...], table_refs[1][...]
        for head in range(heads):
            raw = accs[0][:, head * HD : (head + 1) * HD] * factor
            turned = pltpu.roll(raw, HD // 2, axis=1)
            outs[0][head] = (raw * cosines + turned * sines).astype(narrow)
        outs[1][...] = (accs[1][...] * factor).astype(narrow)
        outs[2][...] = (accs[2][...] * factor).astype(narrow)

    vmem = pl.BlockSpec(memory_space=pltpu.VMEM)
    hbm = pl.BlockSpec(memory_space=pl.ANY)
    shapes = finals if tables else sums
    scratch = [pltpu.VMEM((count, width, w.shape[1]), narrow) for w in weights]
    if tables:
        scratch += [pltpu.VMEM(shape.shape, wide) for shape in sums[:3]]
    scratch += [pltpu.SemaphoreType.DMA((3, count))]
    return pl.pallas_call(
        body,
        out_shape=shapes,
        in_specs=[pl.BlockSpec(memory_space=pltpu.SMEM)]
        + [vmem] * (count + 1)
        + [hbm] * 3
        + [vmem] * (len(carried) + len(tables)),
        out_specs=[vmem] * len(shapes),
        scratch_shapes=scratch,
    )(sources, *chunks, gain, *weights, *carried, *tables)


def attend_and_mix(sequence, query, key_raw, value, cosine, sine, visible, stored, weight):
    index = lax.axis_index("tensor")
    heads, rows = query.shape[0], NEW
    span = slice(sequence * rows, (sequence + 1) * rows)
    devices = len(stored)
    local_tokens = stored[0].shape[2]
    context = devices * local_tokens
    cols = weight.shape[1] // devices
    inner = weight.shape[0]
    root = 1.0 / math.sqrt(HD)

    def body(index_ref, query_ref, key_ref, value_ref, cosine_ref, sine_ref, visible_ref, *refs):
        stored_refs, weight_hbm = refs[:devices], refs[devices]
        outs = refs[devices + 1 : 2 * devices + 1]
        weight_buf, keys, values, mixed, staged, sems, out_sems = refs[2 * devices + 1 :]
        here = index_ref[0]
        order = list(reversed(range(devices)))
        loads = {}
        for slot in order:
            loads[slot] = pltpu.make_async_copy(
                weight_hbm.at[:, pl.ds((here ^ slot) * cols, cols)], weight_buf.at[slot], sems.at[slot]
            )
            loads[slot].start()
        for k in range(devices):
            start = (here ^ k) * local_tokens
            keys[pl.ds(start, local_tokens), :] = stored_refs[k][sequence, 0]
            values[pl.ds(start, local_tokens), :] = stored_refs[k][sequence, 1]
        raw = key_ref[span, :].astype(wide)
        turned = pltpu.roll(raw, HD // 2, axis=1)
        new_key = (raw * cosine_ref[span, :] + turned * sine_ref[span, :]).astype(narrow)
        new_value = value_ref[span, :]
        seen = visible_ref[sequence] > 0
        causal = lax.broadcasted_iota(jnp.int32, (rows, rows), 0) >= lax.broadcasted_iota(
            jnp.int32, (rows, rows), 1
        )
        across = (((1,), (1,)), ((), ()))
        for head in range(heads):
            own = query_ref[head, span, :]
            old = lax.dot_general(own, keys[...], across, preferred_element_type=wide) * root
            old = jnp.where(seen, old, hidden)
            new = lax.dot_general(own, new_key, across, preferred_element_type=wide) * root
            new = jnp.where(causal, new, hidden)
            largest = jnp.maximum(
                jnp.max(old, axis=1, keepdims=True), jnp.max(new, axis=1, keepdims=True)
            )
            old = jnp.exp(old - largest)
            new = jnp.exp(new - largest)
            total = jnp.sum(old, axis=1, keepdims=True) + jnp.sum(new, axis=1, keepdims=True)
            share = 1.0 / total
            mix = jnp.dot((old * share).astype(narrow), values[...], preferred_element_type=wide)
            mix = mix + jnp.dot((new * share).astype(narrow), new_value, preferred_element_type=wide)
            mixed[:, head * HD : (head + 1) * HD] = mix.astype(narrow)
        stores = []
        for slot in order:
            loads[slot].wait()
            product = jnp.dot(mixed[...], weight_buf[slot], preferred_element_type=wide)
            staged[slot] = product.astype(narrow)
            store = pltpu.make_async_copy(staged.at[slot], outs[slot], out_sems.at[slot])
            store.start()
            stores.append(store)
        for store in stores:
            store.wait()

    vmem = pl.BlockSpec(memory_space=pltpu.VMEM)
    hbm = pl.BlockSpec(memory_space=pl.ANY)
    return pl.pallas_call(
        body,
        out_shape=[jax.ShapeDtypeStruct((rows, cols), narrow)] * devices,
        in_specs=[pl.BlockSpec(memory_space=pltpu.SMEM)] + [vmem] * (6 + devices) + [hbm],
        out_specs=[hbm] * devices,
        scratch_shapes=[
            pltpu.VMEM((devices, inner, cols), narrow),
            pltpu.VMEM((context, HD), narrow),
            pltpu.VMEM((context, HD), narrow),
            pltpu.VMEM((rows, inner), narrow),
            pltpu.VMEM((devices, rows, cols), narrow),
            pltpu.SemaphoreType.DMA((devices,)),
            pltpu.SemaphoreType.DMA((devices,)),
        ],
    )(index[None], query, key_raw, value, cosine, sine, visible, *stored, weight)


def place(matched, blocks):
    workers, local_count = len(blocks), len(blocks[0])
    flat = [block for row in blocks for block in row]
    slots = matched.shape[0]
    shape = flat[0].shape

    def body(worker_ref, matched_ref, *refs):
        out, empty, sems = refs[len(flat) :]
        empty[...] = jnp.zeros(shape, empty.dtype)
        for k in range(slots):
            found = jnp.int32(0)
            for shift in range(workers):
                for s in range(local_count):
                    start = (worker_ref[0] - shift + workers) % workers * local_count
                    chosen = matched_ref[k, start + s]
                    found = found + chosen

                    @pl.when(chosen != 0)
                    def _():
                        source = refs[shift * local_count + s]
                        pltpu.make_async_copy(source, out.at[0, k], sems.at[k]).start()

            @pl.when(found == 0)
            def _():
                pltpu.make_async_copy(empty, out.at[0, k], sems.at[k]).start()

        for k in range(slots):
            pltpu.make_async_copy(empty, out.at[0, k], sems.at[k]).wait()

    smem = pl.BlockSpec(memory_space=pltpu.SMEM)
    vmem = pl.BlockSpec(memory_space=pltpu.VMEM)
    return pl.pallas_call(
        body,
        out_shape=jax.ShapeDtypeStruct((1, slots) + shape, flat[0].dtype),
        in_specs=[smem, smem] + [vmem] * len(flat),
        out_specs=pl.BlockSpec(memory_space=pl.ANY),
        scratch_shapes=[pltpu.VMEM(shape, flat[0].dtype), pltpu.SemaphoreType.DMA((slots,))],
        compiler_params=pltpu.CompilerParams(vmem_limit_bytes=4 << 20),
        name="place",
    )(lax.axis_index("worker")[None], matched, *flat)


def attend_on_plane(
    token_rows,
    blocks,
    lengths,
    tables,
    norm_gain,
    query_weight,
    key_weight,
    value_weight,
    output_weight,
):
    count = lax.axis_size("tensor")
    plane = Plane(count)
    seq_count, local_tokens = blocks.shape[0], blocks.shape[1]
    width = token_rows.shape[1]
    logical = tables[:, :, None] * BLK + jnp.arange(BLK, dtype=jnp.int32)
    logical = logical.reshape(seq_count, 1, -1)
    visible = (logical < lengths[:, None, None]).astype(wide)
    positions = (lengths[:, None] + jnp.arange(NEW, dtype=jnp.int32)[None, :]).astype(wide)
    cosine, sine = tables_of(positions)
    gain = norm_gain.reshape(count, 1, width)
    weights = (query_weight, key_weight, value_weight)
    cosine, sine = cosine.reshape(-1, HD), sine.reshape(-1, HD)
    pieces = blocks.reshape(seq_count, local_tokens, 2, count, HD).transpose(3, 0, 2, 1, 4)
    stored = plane.exchange(pieces)
    chunks, order = plane.relay(token_rows)
    sources = lax.axis_index("tensor") ^ order
    half = count // 2
    sums = project(chunks[:half], sources[:half], None, gain, weights, None, None)
    query, key_raw, value = project(
        chunks[half:], sources[half:], sums, gain, weights, cosine, sine
    )
    results = []
    for s in range(seq_count):
        partial = attend_and_mix(
            s, query, key_raw, value, cosine, sine, visible, stored, output_weight
        )
        results.append(plane.scatter(partial))
    return results


def fits_plane(count):
    return count == KVH and count == 2 * 4


def from_partner(block, axis, bit):
    count = lax.axis_size(axis)
    route = []
    for low in range(count):
        high = low | 1 << bit
        if high != low and high < count:
            route += [(low, high), (high, low)]
    return lax.ppermute(block, axis, route)


def rotate(values, positions):
    halfway = HD // 2
    inverse = 500000.0 ** (-(jnp.arange(halfway, dtype=jnp.float32) * 2.0 / HD))
    angles = positions[:, None] * inverse[None, :]
    cosine_table = jnp.concatenate([jnp.cos(angles), jnp.cos(angles)], axis=-1)[:, None, :]
    sine_table = jnp.concatenate([jnp.sin(angles), jnp.sin(angles)], axis=-1)[:, None, :]
    turned = jnp.concatenate([-values[..., halfway:], values[..., :halfway]], axis=-1)
    return values * cosine_table + turned * sine_table


def attend_anywhere(
    token_rows,
    blocks,
    lengths,
    tables,
    norm_gain,
    query_weight,
    key_weight,
    value_weight,
    output_weight,
):
    tensor_count = lax.axis_size("tensor")
    tensor_index = lax.axis_index("tensor")
    group_width = tensor_count // KVH
    bit_count = group_width.bit_length() - 1
    seq_count = blocks.shape[0]
    total = token_rows.shape[0]
    query_cols = query_weight.shape[1]
    widened = lax.all_gather(token_rows, "tensor", axis=1, tiled=True).astype(jnp.float32)
    scaled = (widened * norm_gain[None, :]).astype(jnp.bfloat16)
    query_sum = jnp.dot(scaled, query_weight, preferred_element_type=jnp.float32)
    key_sum = jnp.dot(scaled, key_weight, preferred_element_type=jnp.float32)
    value_sum = jnp.dot(scaled, value_weight, preferred_element_type=jnp.float32)
    squares = jnp.sum(widened * widened, axis=1)
    factor = lax.rsqrt(squares / D + epsilon)[:, None]
    positions = (
        (lengths[:, None] + jnp.arange(NEW, dtype=jnp.int32)[None, :])
        .reshape(total)
        .astype(jnp.float32)
    )
    heads_here = query_cols // HD
    queries = rotate((query_sum * factor).reshape(total, heads_here, HD), positions).astype(
        jnp.bfloat16
    )
    key_full = (key_sum * factor).astype(jnp.bfloat16)
    value_full = (value_sum * factor).astype(jnp.bfloat16)
    for bit in range(bit_count):
        other_key, other_value = from_partner((key_full, value_full), "tensor", bit)
        upper = tensor_index // (1 << bit) % 2 == 1
        key_full = jnp.where(
            upper,
            jnp.concatenate([other_key, key_full], axis=1),
            jnp.concatenate([key_full, other_key], axis=1),
        )
        value_full = jnp.where(
            upper,
            jnp.concatenate([other_value, value_full], axis=1),
            jnp.concatenate([value_full, other_value], axis=1),
        )
    new_key = rotate(key_full.astype(jnp.float32)[:, None, :], positions)[:, 0, :].astype(
        jnp.bfloat16
    )
    fresh_keys = new_key.reshape(seq_count, NEW, HD)
    fresh_values = value_full.reshape(seq_count, NEW, HD)
    local_tokens = blocks.shape[1]
    inverse_root = 1.0 / math.sqrt(HD)
    query_blocks = queries.reshape(seq_count, NEW, heads_here, HD)
    causal = jnp.arange(NEW)[:, None] >= jnp.arange(NEW)[None, :]
    spread = jnp.repeat(
        blocks.reshape(seq_count, local_tokens, 2, KVH, HD), tensor_count // KVH, axis=3
    )
    arrived = lax.all_to_all(spread, "tensor", split_axis=3, concat_axis=1, tiled=True)
    context = arrived.shape[1]
    old_key = arrived[:, :, 0, 0, :]
    old_value = arrived[:, :, 1, 0, :]
    logical = (tables[:, :, None] * BLK + jnp.arange(BLK, dtype=jnp.int32)).reshape(seq_count, context)
    visible = logical < lengths[:, None]
    old_scores = (
        jnp.einsum("sqhd,skd->shqk", query_blocks, old_key, preferred_element_type=jnp.float32)
        * inverse_root
    )
    old_scores = jnp.where(visible[:, None, None, :], old_scores, -1e30)
    new_scores = (
        jnp.einsum("sqhd,skd->shqk", query_blocks, fresh_keys, preferred_element_type=jnp.float32)
        * inverse_root
    )
    new_scores = jnp.where(causal[None, None], new_scores, -1e30)
    largest = jnp.maximum(jnp.max(old_scores, axis=3), jnp.max(new_scores, axis=3))[..., None]
    old_expo = jnp.exp(old_scores - largest)
    new_expo = jnp.exp(new_scores - largest)
    denominator = (jnp.sum(old_expo, axis=3) + jnp.sum(new_expo, axis=3))[..., None]
    old_probs = (old_expo / denominator).astype(jnp.bfloat16)
    new_probs = (new_expo / denominator).astype(jnp.bfloat16)
    mixture = jnp.einsum("shqk,skd->sqhd", old_probs, old_value, preferred_element_type=jnp.float32)
    mixture = mixture + jnp.einsum(
        "shqk,skd->sqhd", new_probs, fresh_values, preferred_element_type=jnp.float32
    )
    attended_rows = mixture.astype(jnp.bfloat16).reshape(total, heads_here * HD)
    partial_value = jnp.dot(attended_rows, output_weight, preferred_element_type=jnp.float32)
    summed = lax.psum_scatter(partial_value, "tensor", scatter_dimension=1, tiled=True)
    finished = summed.astype(jnp.bfloat16).reshape(seq_count, NEW, -1)
    return [finished[s] for s in range(seq_count)]


def local(
    tokens,
    norm_gain,
    query_weight,
    key_weight,
    value_weight,
    output_weight,
    cached_blocks,
    cache_length,
    block_table,
    destination,
):
    worker_index = lax.axis_index("worker")
    worker_count = lax.axis_size("worker")
    seq_total = destination.shape[0]
    belongs = (destination == worker_index).astype(jnp.int32)
    ranking = jnp.sum(jnp.tril(jnp.broadcast_to(belongs, (seq_total, seq_total))), axis=1) - 1
    matched = (belongs[None, :] == 1) & (
        ranking[None, :] == jnp.arange(CAP, dtype=jnp.int32)[:, None]
    )
    matched = matched.astype(jnp.int32)
    local_count = cached_blocks.shape[0]
    first = worker_index * local_count
    run = attend_on_plane if fits_plane(lax.axis_size("tensor")) else attend_anywhere
    own = run(
        tokens,
        cached_blocks,
        lax.dynamic_slice_in_dim(cache_length, first, local_count, 0),
        lax.dynamic_slice_in_dim(block_table, first, local_count, 0),
        norm_gain,
        query_weight,
        key_weight,
        value_weight,
        output_weight,
    )
    blocks = []
    for shift in range(worker_count):
        route = [(w, (w + shift) % worker_count) for w in range(worker_count)]
        row = []
        for s in range(local_count):
            row.append(lax.ppermute(own[s], "worker", route) if shift else own[s])
        blocks.append(row)
    return place(matched, blocks)


def solution(mesh):
    placed = (
        P(("groups", "worker"), "tensor"),
        P(),
        P(None, "tensor"),
        P(None, "tensor"),
        P(None, "tensor"),
        P("tensor", None),
        P(("groups", "worker"), "tensor", None, None),
        P("groups"),
        P("groups", None),
        P("groups"),
    )

    return jax.shard_map(
        local,
        mesh=mesh,
        in_specs=placed,
        out_specs=P(("groups", "worker"), None, None, "tensor"),
        check_vma=False,
    )
```
